32 devices in a mesh: row: 2 (over core), col: 8 (over z, y), layer: 2 (over x).
Axes of the slice: x: 2, y: 2, z: 4, core: 2. Of those that a mesh axis runs over, the one named last changes fastest.
Arguments:
- blocks: float32 [128, 8, 128, 128], P(('row', 'col')), may hold values from -0.375 to 0.375
- columns: int32 [128, 8], replicated, may hold values from 0 to 127, as said below
- row_order: int32 [128], replicated, may hold values from 0 to 127, as said below
Outputs:
- new_blocks: float32 [128, 8, 128, 128], P(('row', 'col'), 'layer')
The draws below stay inside these ranges and needn't reach their ends.
Inputs may be any that keep to these rules, and one draw needn't show every extreme that they name: Row p names 8 different block columns, one of them row_order[p]; each is row_order[q] for a position q within a cyclic distance of 8 of p over the 128 positions; the first position of each aligned group of 8 names the position 8 back, the last names the position 8 ahead. `row_order`: every block row once.
All inputs are finite; a program needn't handle non-finite values.
Results may differ from the reference program's by a relative error of at most 0.0003.
Values sent between devices are 32-bit elements; how exact they have to be, the bound alone decides.
No kernel may reach another device: no remote copies, remote signals or barrier semaphores. Data moves between devices by JAX's collectives and lax.ppermute only.
A program may use at most 128 MiB of HBM per device.

```python
import jax
import jax.numpy as jnp
from jax import lax

BLK = 128
SLOTS = 8
ROWS_DEV = 8
NBLK = 128


def pattern_parts(key):
    ordering = jax.random.permutation(jax.random.fold_in(key, 11), NBLK).astype(jnp.int32)
    span_count = 2 * ROWS_DEV + 1
    scores = jax.random.randint(jax.random.fold_in(key, 12), (NBLK, span_count), 0, 65536) * span_count + jnp.arange(span_count)
    places = jnp.arange(NBLK)
    scores = scores.at[:, ROWS_DEV].set(-3)
    scores = scores.at[:, 0].set(jnp.where(places % ROWS_DEV == 0, -2, scores[:, 0]))
    scores = scores.at[:, span_count - 1].set(jnp.where(places % ROWS_DEV == ROWS_DEV - 1, -1, scores[:, span_count - 1]))
    chosen = jnp.argsort(scores, axis=1)[:, :SLOTS]
    shuffle = jax.random.randint(jax.random.fold_in(key, 13), (NBLK, SLOTS), 0, 65536) * SLOTS + jnp.arange(SLOTS)
    slot_order = jnp.argsort(shuffle, axis=1)
    offsets = jnp.take_along_axis(chosen, slot_order, axis=1) - ROWS_DEV
    targets = (places[:, None] + offsets) % NBLK
    return (ordering, ordering[targets].astype(jnp.int32))


def draw_columns(key, part):
    return pattern_parts(key)[1]


def draw_row_order(key, part):
    return pattern_parts(key)[0]


def levels(stream_key, dims, split, smallest, high):
    def one(dim, parts):
        heights = jax.random.uniform(jax.random.fold_in(jax.random.fold_in(stream_key, 6), dim), (parts,), jnp.float32, smallest / len(split), high / len(split))
        return jnp.repeat(jnp.exp(heights), dims[dim] // parts).reshape((-1,) + (1,) * (len(dims) - dim - 1))

    loudness = one(*split[0])
    for cut in split[1:]:
        loudness = loudness * one(*cut)
    return loudness


def scatter_about(stream_key, dims, width, most, split=(), kind=jnp.bfloat16):
    result = width * jax.random.normal(stream_key, dims, jnp.float32)
    if split:
        result = result * levels(stream_key, dims, split, -0.22, 0.18)
    return jnp.clip(result, -most, most).astype(kind)


def setup_inputs(seed: int = 0) -> dict:
    key_list = jax.random.split(jax.random.key(seed), 4)
    blocks = scatter_about(key_list[0], (NBLK, SLOTS, BLK, BLK), (2 * BLK) ** -0.5, 0.375, ((0, 16),), jnp.float32)
    columns = draw_columns(jax.random.fold_in(key_list[3], 71), 0)
    row_order = draw_row_order(jax.random.fold_in(key_list[3], 71), 0)
    return {"blocks": blocks, "columns": columns, "row_order": row_order}


def restricted_product(left, right, columns, located):
    def one_row(index):
        left_row = left[index]
        targets = located[index]
        right_rows = right[targets]
        right_cols = columns[targets]
        matches = (columns[index][:, None, None] == right_cols[None, :, :]).astype(left.dtype)
        products = jnp.einsum("axy,atyz->atxz", left_row, right_rows, precision=lax.Precision.HIGHEST)
        return jnp.einsum("sat,atxz->sxz", matches, products, precision=lax.Precision.HIGHEST)

    return lax.map(one_row, jnp.arange(left.shape[0], dtype=jnp.int32))


def reference(blocks, columns, row_order):
    total_rows = row_order.shape[0]
    position = jnp.zeros((total_rows,), jnp.int32).at[row_order].set(jnp.arange(total_rows, dtype=jnp.int32))
    located = position[columns]
    square = restricted_product(blocks, blocks, columns, located)
    cube = restricted_product(square, blocks, columns, located)
    return 1.5 * blocks - 0.5 * cube
```

```python
import functools

import jax
import jax.numpy as jnp
from jax import lax
from jax.experimental import pallas as pl
from jax.experimental.pallas import tpu as pltpu
from jax.sharding import PartitionSpec as P

AXES = ("row", "col", "layer")
CHUNKS = ((0, 2), (2, 2), (4, 2), (6, 2))
ANY = pl.BlockSpec(memory_space=pl.ANY)
SMEM = pl.BlockSpec(memory_space=pltpu.SMEM)
F32 = jnp.float32
BF16 = jnp.bfloat16


def dot(a, b):
    return jnp.dot(a, b, preferred_element_type=F32)


def halves(x):
    high = x.astype(BF16)
    return high, (x - high.astype(F32)).astype(BF16)


def multiply_pair(left_high, left_low, right_high, right_low, total, slots, pair):
    width = 256
    for part in range(right_high.shape[-1] // width):
        lanes = slice(part * width, (part + 1) * width)
        high, low = right_high[:, lanes], right_low[:, lanes]
        terms = dot(left_high, high) + (dot(left_low, high) + dot(left_high, low))
        for k in range(2):
            slot = slots[pair, 2 * part + k]
            total[slot] += terms[:, k * 128 : (k + 1) * 128]


def split_row(source, high, low):
    for t in range(source.shape[0]):
        lanes = slice(t * 128, (t + 1) * 128)
        high[:, lanes], low[:, lanes] = halves(source[t])


def own_kernel(meta, where, slots, blocks, total_out, staged, left_high, left_low, high, low, total, sems, out_sems):
    rows, width = blocks.shape[0], blocks.shape[1]

    @pl.when(meta[0] == 1)
    def _():
        copies = [pltpu.make_async_copy(blocks.at[i], staged.at[i], sems.at[i]) for i in range(rows)]
        for copy in copies:
            copy.start()

        def zero(i, _):
            for s in range(width + 1):
                total[i, s] = jnp.zeros((128, 128), F32)
            return 0

        lax.fori_loop(0, rows, zero, 0)

        def prepare(i, _):
            pltpu.make_async_copy(blocks.at[i], staged.at[i], sems.at[i]).wait()
            split_row(staged.at[i], high.at[i], low.at[i])
            for t in range(width):
                lanes = slice(t * 128, (t + 1) * 128)
                left_high[i, t] = high[i, :, lanes]
                left_low[i, t] = low[i, :, lanes]
            return 0

        lax.fori_loop(0, rows, prepare, 0)

        def row(i, _):
            def pair(a, _):
                n = i * width + a
                w = where[n]

                @pl.when((w >= rows) & (w < 2 * rows))
                def _():
                    v = w - rows
                    multiply_pair(left_high[i, a], left_low[i, a], high.at[v], low.at[v], total.at[i], slots, n)

                return 0

            lax.fori_loop(0, width, pair, 0)
            pltpu.make_async_copy(total.at[i, pl.ds(0, width)], total_out.at[i], out_sems.at[i]).start()
            return 0

        lax.fori_loop(0, rows, row, 0)
        for i in range(rows):
            pltpu.make_async_copy(total.at[i, pl.ds(0, width)], total_out.at[i], out_sems.at[i]).wait()


def last_kernel(
    chunks, meta, where, slots, blocks, total_in, *rest
):
    arrived = rest[: 2 * len(chunks)]
    (mine, other, staged, own, left_high, left_low, high, low, total, cube, sems, own_sems, total_sems, out_sems) = rest[2 * len(chunks) :]
    rows, width = blocks.shape[0], blocks.shape[1]
    share = width // 2
    odd = meta[1]
    layer = meta[2]

    @pl.when(meta[0] == 1)
    def _():
        copies = []
        for i in range(rows):
            copies.append((pltpu.make_async_copy(blocks.at[i], own.at[i], own_sems.at[i]), None))
        for i in range(rows):
            copies.append((pltpu.make_async_copy(total_in.at[i], total.at[i, pl.ds(0, width)], total_sems.at[i]), None))
        landed = []
        for k, (start, size) in enumerate(chunks):
            for source, hop in ((arrived[k], 0), (arrived[len(chunks) + k], 1)):
                for r in range(size):
                    even_row, odd_row = start + r, rows - start - size + r
                    base_odd, base_even = (0, 2 * rows) if hop == 0 else (2 * rows, 0)
                    w = jnp.where(odd == 1, base_odd + even_row, base_even + odd_row)
                    place = jnp.where(w >= 2 * rows, w - rows, w)
                    n = len(landed)
                    landed.append((pltpu.make_async_copy(source.at[r], staged.at[place], sems.at[n]), w, place))
        for copy, _ in copies:
            copy.start()
        for copy, _, _ in landed:
            copy.start()

        def prepare(i, _):
            pltpu.make_async_copy(blocks.at[i], own.at[i], own_sems.at[i]).wait()
            split_row(own.at[i], high.at[rows + i], low.at[rows + i])
            for t in range(width):
                lanes = slice(t * 128, (t + 1) * 128)
                left_high[i, t] = high[rows + i, :, lanes]
                left_low[i, t] = low[rows + i, :, lanes]
            return 0

        lax.fori_loop(0, rows, prepare, 0)
        for copy, _, _ in landed:
            copy.wait()

        def prepare_far(place, _):
            w = jnp.where(place >= rows, place + rows, place)
            split_row(staged.at[place], high.at[w], low.at[w])
            return 0

        lax.fori_loop(0, 2 * rows, prepare_far, 0)

        def row(i, _):
            pltpu.make_async_copy(total_in.at[i], total.at[i, pl.ds(0, width)], total_sems.at[i]).wait()

            def pair(a, _):
                n = i * width + a
                w = where[n]

                @pl.when((w < rows) | (w >= 2 * rows))
                def _():
                    multiply_pair(left_high[i, a], left_low[i, a], high.at[w], low.at[w], total.at[i], slots, n)

                return 0

            lax.fori_loop(0, width, pair, 0)
            for s in range(width):
                left_high[i, s], left_low[i, s] = halves(total[i, s])
                cube[i, s] = jnp.zeros((128, 128), F32)

            def pair_cube(a, _):
                n = i * width + a
                w = where[n]
                multiply_pair(left_high[i, a], left_low[i, a], high.at[w], low.at[w], cube.at[i], slots, n)
                return 0

            lax.fori_loop(0, width, pair_cube, 0)
            for s in range(width):
                cube[i, s] = 1.5 * own[i, s] - 0.5 * cube[i, s]
            pltpu.make_async_copy(cube.at[i, pl.ds(layer * share, share)], mine.at[i], out_sems.at[i]).start()
            pltpu.make_async_copy(cube.at[i, pl.ds((1 - layer) * share, share)], other.at[i], out_sems.at[rows + i]).start()
            return 0

        lax.fori_loop(0, rows, row, 0)
        for i in range(rows):
            pltpu.make_async_copy(cube.at[i, pl.ds(layer * share, share)], mine.at[i], out_sems.at[i]).wait()
            pltpu.make_async_copy(cube.at[i, pl.ds((1 - layer) * share, share)], other.at[i], out_sems.at[rows + i]).wait()


def on_device(cols_n, layers, blocks, columns, row_order):
    rows, width = blocks.shape[0], blocks.shape[1]
    total_rows = row_order.shape[0]
    n = 2 * cols_n
    vmem = functools.partial(pltpu.VMEM)

    def device(r, j, l):
        return (r * cols_n + j) * layers + l

    def owner(c):
        l, j = divmod(c % n, cols_n)
        return device(l, j, l)

    near = [(owner(c), owner(c ^ 1)) for c in range(n)]
    relay = [(owner(c), owner(c + 2 if c % 2 == 0 else c - 2)) for c in range(n)]
    across = [(device(l, j, l), device(l, j, 1 - l)) for j in range(cols_n) for l in range(2)]

    r, j, l = (lax.axis_index(a) for a in AXES)
    segment = r * cols_n + j
    odd = segment % 2
    is_owner = (r == l).astype(jnp.int32)

    arrived_near, arrived_far = [], []
    for start, size in CHUNKS:
        first = jnp.where(odd == 1, rows - start - size, start)
        arrived_near.append(lax.ppermute(lax.dynamic_slice_in_dim(blocks, first, size, 0), AXES, near))
    for piece in arrived_near:
        arrived_far.append(lax.ppermute(piece, AXES, relay))

    window = (segment * rows - rows + jnp.arange(3 * rows, dtype=jnp.int32)) % total_rows
    window_order, window_cols = row_order[window], columns[window]
    own_cols = lax.dynamic_slice_in_dim(columns, segment * rows, rows, 0)
    same = own_cols[:, :, None] == window_order[None, None, :]
    where = jnp.sum(jnp.where(same, jnp.arange(3 * rows, dtype=jnp.int32), 0), axis=2).reshape(-1)
    named = window_cols[where].reshape(rows, width, width)
    match = named[:, :, :, None] == own_cols[:, None, None, :]
    slots = width + jnp.sum(jnp.where(match, jnp.arange(width, dtype=jnp.int32) - width, 0), axis=3)
    slots = slots.reshape(rows * width, width)
    meta = jnp.stack([is_owner, odd, l]).astype(jnp.int32)

    limit = pltpu.CompilerParams(vmem_limit_bytes=60 * 1024 * 1024)
    block = (128, 128)
    total = pl.pallas_call(
        own_kernel,
        out_shape=jax.ShapeDtypeStruct(blocks.shape, F32),
        in_specs=[SMEM, SMEM, SMEM, ANY],
        out_specs=ANY,
        scratch_shapes=[
            vmem((rows, width) + block, F32),
            vmem((rows, width) + block, BF16),
            vmem((rows, width) + block, BF16),
            vmem((rows, 128, width * 128), BF16),
            vmem((rows, 128, width * 128), BF16),
            vmem((rows, width + 1) + block, F32),
            pltpu.SemaphoreType.DMA((rows,)),
            pltpu.SemaphoreType.DMA((rows,)),
        ],
        compiler_params=limit,
        name="own_part",
    )(meta, where, slots, blocks)

    half = jax.ShapeDtypeStruct((rows, width // 2) + block, F32)
    mine, other = pl.pallas_call(
        functools.partial(last_kernel, CHUNKS),
        out_shape=(half, half),
        in_specs=[SMEM, SMEM, SMEM, ANY, ANY] + [ANY] * (2 * len(CHUNKS)),
        out_specs=(ANY, ANY),
        scratch_shapes=[
            vmem((2 * rows, width) + block, F32),
            vmem((rows, width) + block, F32),
            vmem((rows, width) + block, BF16),
            vmem((rows, width) + block, BF16),
            vmem((3 * rows, 128, width * 128), BF16),
            vmem((3 * rows, 128, width * 128), BF16),
            vmem((rows, width + 1) + block, F32),
            vmem((rows, width + 1) + block, F32),
            pltpu.SemaphoreType.DMA((2 * rows,)),
            pltpu.SemaphoreType.DMA((rows,)),
            pltpu.SemaphoreType.DMA((rows,)),
            pltpu.SemaphoreType.DMA((2 * rows,)),
        ],
        compiler_params=limit,
        name="last_part",
    )(meta, where, slots, blocks, total, *arrived_near, *arrived_far)
    received = lax.ppermute(other, AXES, across)
    return jnp.where(is_owner == 1, mine, received)


def solution(mesh):
    assert mesh.shape["row"] == 2 and mesh.shape["layer"] == 2
    placed = (P(("row", "col"), None, None, None), P(), P())
    return jax.shard_map(
        functools.partial(on_device, mesh.shape["col"], mesh.shape["layer"]),
        mesh=mesh,
        in_specs=placed,
        out_specs=P(("row", "col"), "layer", None, None),
        check_vma=False,
    )
```

```python
import functools

import jax
import jax.numpy as jnp
from jax import lax
from jax.experimental import pallas as pl
from jax.experimental.pallas import tpu as pltpu
from jax.sharding import PartitionSpec as P


AXES = ("row", "col", "layer")
PIECES = 4
STAGE_GROUP, PART_GROUP, CUBE_GROUP = 16, 8, 18
ANY = pl.BlockSpec(memory_space=pl.ANY)
SMEM = pl.BlockSpec(memory_space=pltpu.SMEM)
VMEM = pl.BlockSpec(memory_space=pltpu.VMEM)
F32 = jnp.float32
BF16 = jnp.bfloat16
NEAR, FAR = 0, 1


def halves(x):
    high = x.astype(BF16)
    return high, (x - high.astype(F32)).astype(BF16)


def lanes(t):
    if isinstance(t, int):
        return slice(t * 128, (t + 1) * 128)
    return pl.ds(pl.multiple_of(t * 128, 128), 128)


def split_row(source, high, low):
    for t in range(source.shape[0]):
        high[:, lanes(t)], low[:, lanes(t)] = halves(source[t])


def clear(total):
    def one(i, _):
        for s in range(total.shape[1]):
            total[i, s] = jnp.zeros(total.shape[2:], F32)
        return 0

    lax.fori_loop(0, total.shape[0], one, 0)


def add_pairs(group, sources, span, tables, todo, left, high, low, total, first=0):
    _, where, kinds, needed, blocks_of = tables
    width = total.shape[1] - 1
    twos = width // 2
    pairs = kinds.shape[0]
    start, length = span
    mask = None if sources is None else sum(1 << x for x in sources)

    def list_one(k, count):
        n = start * width + k
        for p in range(twos):
            todo[count + p] = n * twos + p
        more = needed[n]
        return count + (more if mask is None else ((mask >> kinds[n]) & 1) * more)

    count = lax.fori_loop(0, length * width, list_one, jnp.int32(0), unroll=8)
    for k in range(group):
        todo[count + k] = pairs * twos

    def some(m, _):
        for k in range(group):
            entry = todo[m * group + k]
            n = entry // twos
            i = jnp.clip(n // width - first, 0, total.shape[0] - 1)
            w = where[n]
            codes = [blocks_of[2 * entry + e] for e in range(2)]
            left_high, left_low = left(i, n % width)
            right = [jnp.concatenate([x[w, :, lanes(c // 16)] for c in codes], axis=1) for x in (high, low)]
            terms = jnp.dot(
                jnp.concatenate([left_high, left_low, left_high], axis=1),
                jnp.concatenate([right[0], right[0], right[1]], axis=0),
                preferred_element_type=F32,
            )
            for e in range(2):
                total[i, codes[e] % 16] += terms[:, lanes(e)]
        return 0

    lax.fori_loop(0, (count + group - 1) // group, some, 0)


def window_row(odd, rows, hop, begin, r):
    size = rows // PIECES
    ascending, descending = begin * size + r, rows - (begin + 1) * size + r
    before, after = (ascending, 2 * rows + descending) if hop == NEAR else (descending, 2 * rows + ascending)
    return jnp.where(odd == (1 if hop == NEAR else 0), before, after)


def cut_kernel(pieces, meta, blocks, *rest):
    outs, sems = rest[: len(pieces)], rest[len(pieces)]
    rows = blocks.shape[0]
    size = rows // PIECES

    @pl.when(meta[0] == 1)
    def _():
        copies = []
        for k, (piece, out) in enumerate(zip(pieces, outs)):
            begin = jnp.where(meta[1] == 1, rows - (piece + 1) * size, piece * size)
            copies.append(pltpu.make_async_copy(blocks.at[pl.ds(begin, size)], out, sems.at[k]))
        for copy in copies:
            copy.start()
        for copy in copies:
            copy.wait()


def own_left(high, low, rows):
    return lambda i, a: (high[rows + i, :, lanes(a)], low[rows + i, :, lanes(a)])


def own_kernel(meta, where, kinds, needed, blocks_of, blocks, high, low, total, staged, todo, sems):
    rows = blocks.shape[0]
    tables = (meta, where, kinds, needed, blocks_of)

    @pl.when(meta[0] == 1)
    def _():
        for i in range(rows):
            pltpu.make_async_copy(blocks.at[i], staged.at[i], sems.at[i]).start()
        clear(total)

        def prepare(i, _):
            pltpu.make_async_copy(blocks.at[i], staged.at[i], sems.at[i]).wait()
            split_row(staged.at[i], high.at[rows + i], low.at[rows + i])
            return 0

        lax.fori_loop(0, rows, prepare, 0)
        add_pairs(STAGE_GROUP, (0,), (0, rows), tables, todo, own_left(high, low, rows), high, low, total)


def take_in(pieces, arrived, odd, rows, high, low):
    for (hop, begin), source in zip(pieces, arrived):
        def one(r, _):
            w = window_row(odd, rows, hop, begin, r)
            split_row(source.at[r], high.at[w], low.at[w])
            return 0

        lax.fori_loop(0, source.shape[0], one, 0)


def stage_kernel(sources, pieces, rows, *refs):
    tables, arrived = refs[:5], refs[5 : 5 + len(pieces)]
    high, low, total, todo = refs[5 + len(pieces) + 3 :]

    @pl.when(tables[0][0] == 1)
    def _():
        take_in(pieces, arrived, tables[0][1], rows, high, low)
        add_pairs(STAGE_GROUP, sources, (0, rows), tables, todo, own_left(high, low, rows), high, low, total)


def final_kernel(sources, pieces, part, *refs):
    tables, blocks, arrived = refs[:5], refs[5], refs[6 : 6 + len(pieces)]
    rest = refs[6 + len(pieces) + (3 if part == 0 else 4) :]
    high, low, total, output, other, own, cube, keep, sq_high, sq_low, todo, sems, out_sems = rest
    rows, width = blocks.shape[0], blocks.shape[1]
    count, share = rows // PIECES, width // 2
    meta = tables[0]
    odd, layer = meta[1], meta[2]
    first = jnp.where(odd == 1, part * count, rows - (part + 1) * count)

    @pl.when(meta[0] == 1)
    def _():
        load = pltpu.make_async_copy(blocks.at[pl.ds(first, count)], own, sems)
        load.start()
        clear(cube)
        take_in(pieces, arrived, odd, rows, high, low)
        add_pairs(PART_GROUP, sources, (first, count), tables, todo, own_left(high, low, rows), high, low, total)
        for i in range(count):
            for s in range(width):
                sq_high[i, s], sq_low[i, s] = halves(total[first + i, s])
        add_pairs(
            CUBE_GROUP, None, (first, count), tables, todo,
            lambda i, a: (sq_high[i, a], sq_low[i, a]), high, low, cube, first,
        )
        load.wait()
        for i in range(count):
            for s in range(share):
                g = layer * share + s
                keep[i, s] = 1.5 * own[i, g] - 0.5 * cube[i, g]
        store = pltpu.make_async_copy(keep, output.at[pl.ds(first, count)], out_sems)
        store.start()
        for i in range(count):
            for s in range(share):
                g = (1 - layer) * share + s
                other[i, s] = 1.5 * own[i, g] - 0.5 * cube[i, g]
        store.wait()


def place_kernel(part, meta, received, output_in, output, sem):
    rows = output.shape[0]
    count = rows // PIECES
    first = jnp.where(meta[1] == 1, part * count, rows - (part + 1) * count)

    @pl.when(meta[0] == 0)
    def _():
        copy = pltpu.make_async_copy(received, output.at[pl.ds(first, count)], sem)
        copy.start()
        copy.wait()


def on_device(cols_n, layers, blocks, columns, row_order):
    rows, width = blocks.shape[0], blocks.shape[1]
    total_rows = row_order.shape[0]
    n = 2 * cols_n
    size = rows // PIECES
    block = (128, 128)
    in_vmem = lambda x: pltpu.with_memory_space_constraint(x, pltpu.VMEM)
    limit = functools.partial(pltpu.CompilerParams, vmem_limit_bytes=20 * 1024 * 1024)

    def device(r, j, l):
        return (r * cols_n + j) * layers + l

    turn = cols_n // 2 // 2 * 2

    def owner(c, other=0):
        r, j = divmod(c % n, cols_n)
        return device(r, j, r ^ (j > turn) ^ other)

    near = [(owner(c), owner(c ^ 1)) for c in range(n)]
    relay = [(owner(c), owner(c + 2 if c % 2 == 0 else c - 2)) for c in range(n)]
    across = [(owner(c), owner(c, 1)) for c in range(n)]

    r, j, l = (lax.axis_index(a) for a in AXES)
    segment = r * cols_n + j
    odd = segment % 2
    is_owner = ((r == l) != (j > turn)).astype(jnp.int32)
    meta = jnp.stack([is_owner, odd, l]).astype(jnp.int32)
    held = pltpu.with_memory_space_constraint(blocks, pltpu.HBM)

    def cut(pieces):
        return pl.pallas_call(
            functools.partial(cut_kernel, pieces),
            out_shape=tuple(pltpu.VMEM((size, width) + block, F32) for _ in pieces),
            in_specs=[SMEM, ANY],
            out_specs=(VMEM,) * len(pieces),
            scratch_shapes=[pltpu.SemaphoreType.DMA((len(pieces),))],
            compiler_params=limit(),
        )(meta, held)

    first_piece = lax.dynamic_slice_in_dim(blocks, jnp.where(odd == 1, rows - size, 0), size, 0)
    cuts = (first_piece,) + tuple(cut(tuple(range(1, PIECES))))
    arrived = {}
    for k in range(PIECES):
        arrived[NEAR, k] = lax.ppermute(cuts[k], AXES, near)
    for k in range(PIECES):
        arrived[FAR, k] = lax.ppermute(arrived[NEAR, k], AXES, relay)

    columns, row_order, arrived[NEAR, 0] = lax.optimization_barrier((columns, row_order, arrived[NEAR, 0]))
    index = jnp.arange(width, dtype=jnp.int32)
    window = (segment * rows - rows + jnp.arange(3 * rows, dtype=jnp.int32)) % total_rows
    window_order, window_cols = row_order[window], columns[window]
    own_cols = lax.dynamic_slice_in_dim(columns, segment * rows, rows, 0)
    same = own_cols[:, :, None] == window_order[None, None, :]
    where = jnp.sum(jnp.where(same, jnp.arange(3 * rows, dtype=jnp.int32), 0), axis=2).reshape(-1)
    named = window_cols[where].reshape(rows, width, width)
    match = named[:, :, :, None] == own_cols[:, None, None, :]
    slots = width + jnp.sum(jnp.where(match, index - width, 0), axis=3).reshape(rows * width, width)
    has = (slots < width).astype(jnp.int32)
    matched = jnp.sum(has, axis=1)
    earlier = jnp.sum(jnp.where(index[None, :, None] > index[None, None, :], has[:, None, :], 0), axis=2)
    rank = jnp.where(has == 1, earlier, matched[:, None] + index - earlier)
    code = 16 * index + slots
    ranked = jnp.sum(jnp.where(rank[:, :, None] == index, code[:, :, None], 0), axis=1)
    blocks_of = jnp.concatenate([ranked.reshape(-1), jnp.full((width,), width, jnp.int32)]).astype(jnp.int32)
    needed = ((matched + 1) // 2).astype(jnp.int32)
    is_own = (where >= rows) & (where < 2 * rows)
    is_near = (where < rows) == (odd == 1)
    inside = where % rows
    piece = jnp.where(odd == 1, inside, rows - 1 - inside) // size
    kinds = jnp.where(is_own, 0, 1 + piece + jnp.where(is_near, 0, PIECES))
    kinds = kinds.astype(jnp.int32)
    where = jnp.concatenate([where, jnp.full((1,), rows, jnp.int32)]).astype(jnp.int32)
    tables = (meta, where, kinds, needed, blocks_of)

    todo = pltpu.SMEM((rows * width * width // 2 + max(STAGE_GROUP, CUBE_GROUP) + width // 2,), jnp.int32)
    state = (
        pltpu.VMEM((3 * rows, 128, width * 128), BF16),
        pltpu.VMEM((3 * rows, 128, width * 128), BF16),
        pltpu.VMEM((rows, width + 1) + block, F32),
    )
    carried = pl.pallas_call(
        own_kernel,
        out_shape=state,
        in_specs=[SMEM] * 5 + [ANY],
        out_specs=(VMEM,) * 3,
        scratch_shapes=[pltpu.VMEM((rows, width) + block, F32), todo, pltpu.SemaphoreType.DMA((rows,))],
        compiler_params=limit(),
        name="own_part",
    )(*tables, held)

    def stage(carried, items):
        m = len(items)
        sources = tuple(1 + k + hop * PIECES for hop, k in items)
        return pl.pallas_call(
            functools.partial(stage_kernel, sources, tuple(items), rows),
            out_shape=state,
            in_specs=[SMEM] * 5 + [VMEM] * (m + 3),
            out_specs=(VMEM,) * 3,
            input_output_aliases={5 + m: 0, 6 + m: 1, 7 + m: 2},
            scratch_shapes=[todo],
            compiler_params=limit(),
        )(*tables, *(in_vmem(arrived[item]) for item in items), *(in_vmem(x) for x in carried))

    def final(carried, items, sources, part, output):
        m = len(items)
        aliases = {6 + m: 0, 7 + m: 1, 8 + m: 2}
        more = ()
        if output is not None:
            aliases[9 + m] = 3
            more = (output,)
        results = pl.pallas_call(
            functools.partial(final_kernel, sources, tuple(items), part),
            out_shape=state
            + (
                jax.ShapeDtypeStruct((rows, width // 2) + block, F32),
                pltpu.VMEM((size, width // 2) + block, F32),
            ),
            in_specs=[SMEM] * 5 + [ANY] + [VMEM] * (m + 3) + [ANY] * len(more),
            out_specs=(VMEM,) * 3 + (ANY, VMEM),
            input_output_aliases=aliases,
            scratch_shapes=[
                pltpu.VMEM((size, width) + block, F32),
                pltpu.VMEM((size, width + 1) + block, F32),
                pltpu.VMEM((size, width // 2) + block, F32),
                pltpu.VMEM((size, width) + block, BF16),
                pltpu.VMEM((size, width) + block, BF16),
                todo,
                pltpu.SemaphoreType.DMA,
                pltpu.SemaphoreType.DMA,
            ],
            compiler_params=limit(),
        )(*tables, held, *(in_vmem(arrived[item]) for item in items), *(in_vmem(x) for x in carried), *more)
        return results[:3], results[3], results[4]

    carried = stage(carried, [(NEAR, 0), (NEAR, 1), (NEAR, 2), (FAR, 0)])
    output, got = None, []
    for part in range(PIECES):
        items = [(NEAR, PIECES - 1)] if part == 0 else [(FAR, part)]
        sources = (PIECES,) + tuple(1 + PIECES + k for k in range(1, part + 1))
        carried, output, give = final(carried, items, sources, part, output)
        got.append(lax.ppermute(give, AXES, across))
    for part in range(PIECES):
        output = pl.pallas_call(
            functools.partial(place_kernel, part),
            out_shape=jax.ShapeDtypeStruct(output.shape, F32),
            in_specs=[SMEM, VMEM, ANY],
            out_specs=ANY,
            input_output_aliases={2: 0},
            scratch_shapes=[pltpu.SemaphoreType.DMA],
            compiler_params=limit(),
        )(meta, in_vmem(got[part]), output)
    return output


def solution(mesh):
    assert mesh.shape["row"] == 2 and mesh.shape["layer"] == 2
    placed = (P(("row", "col"), None, None, None), P(), P())

    def body(*args):
        return on_device(mesh.shape["col"], mesh.shape["layer"], *args)

    return jax.shard_map(
        body,
        mesh=mesh,
        in_specs=placed,
        out_specs=P(("row", "col"), "layer", None, None),
        check_vma=False,
    )
```

```python
import functools

import jax
import jax.numpy as jnp
from jax import lax
from jax.experimental import pallas as pl
from jax.experimental.pallas import tpu as pltpu
from jax.sharding import PartitionSpec as P


AXES = ("row", "col", "layer")
PIECES = 4
STAGE_GROUP, PART_GROUP, CUBE_GROUP = 16, 12, 18
ANY = pl.BlockSpec(memory_space=pl.ANY)
SMEM = pl.BlockSpec(memory_space=pltpu.SMEM)
VMEM = pl.BlockSpec(memory_space=pltpu.VMEM)
F32 = jnp.float32
BF16 = jnp.bfloat16
NEAR, FAR = 0, 1


def halves(x):
    high = x.astype(BF16)
    return high, (x - high.astype(F32)).astype(BF16)


def lanes(t):
    if isinstance(t, int):
        return slice(t * 128, (t + 1) * 128)
    return pl.ds(pl.multiple_of(t * 128, 128), 128)


def split_row(source, high, low):
    for t in range(source.shape[0]):
        high[:, lanes(t)], low[:, lanes(t)] = halves(source[t])


def clear(total):
    def one(i, _):
        for s in range(total.shape[1]):
            total[i, s] = jnp.zeros(total.shape[2:], F32)
        return 0

    lax.fori_loop(0, total.shape[0], one, 0)


def add_pairs(group, sources, span, tables, todo, left, high, low, total, first=0):
    _, where, kinds, needed, blocks_of = tables
    width = total.shape[1] - 1
    twos = width // 2
    pairs = kinds.shape[0]
    start, length = span
    mask = None if sources is None else sum(1 << x for x in sources)

    def list_one(k, count):
        n = start * width + k
        for p in range(twos):
            todo[count + p] = n * twos + p
        more = needed[n]
        return count + (more if mask is None else ((mask >> kinds[n]) & 1) * more)

    count = lax.fori_loop(0, length * width, list_one, jnp.int32(0), unroll=8)
    for k in range(group):
        todo[count + k] = pairs * twos

    def some(m, _):
        for k in range(group):
            entry = todo[m * group + k]
            n = entry // twos
            i = jnp.clip(n // width - first, 0, total.shape[0] - 1)
            w = where[n]
            codes = [blocks_of[2 * entry + e] for e in range(2)]
            left_high, left_low = left(i, n % width)
            right = [jnp.concatenate([x[w, :, lanes(c // 16)] for c in codes], axis=1) for x in (high, low)]
            terms = jnp.dot(
                jnp.concatenate([left_high, left_low, left_high], axis=1),
                jnp.concatenate([right[0], right[0], right[1]], axis=0),
                preferred_element_type=F32,
            )
            for e in range(2):
                total[i, codes[e] % 16] += terms[:, lanes(e)]
        return 0

    lax.fori_loop(0, (count + group - 1) // group, some, 0)


def window_row(odd, rows, hop, begin, r):
    size = rows // PIECES
    ascending, descending = begin * size + r, rows - (begin + 1) * size + r
    before, after = (ascending, 2 * rows + descending) if hop == NEAR else (descending, 2 * rows + ascending)
    return jnp.where(odd == (1 if hop == NEAR else 0), before, after)


def piece_begin(meta, rows, piece):
    size = rows // PIECES
    return jnp.where(meta[1] == 1, rows - (piece + 1) * size, piece * size)


def first_kernel(meta, blocks, out, sem):
    @pl.when(meta[3] == 1)
    def _():
        begin = piece_begin(meta, blocks.shape[0], 0)
        copy = pltpu.make_async_copy(blocks.at[pl.ds(begin, out.shape[0])], out, sem)
        copy.start()
        copy.wait()


def cut_kernel(meta, blocks, first, *rest):
    outs, (staged, in_sems, out_sems) = rest[: PIECES - 1], rest[PIECES - 1 :]
    rows = blocks.shape[0]
    size = rows // PIECES

    @pl.when(meta[3] == 1)
    def _():
        steps = []
        for k, out in enumerate(outs):
            begin = piece_begin(meta, rows, k + 1)
            for r in range(size):
                n = k * size + r
                steps.append(
                    (
                        pltpu.make_async_copy(blocks.at[begin + r], staged.at[n], in_sems.at[n]),
                        pltpu.make_async_copy(staged.at[n], out.at[r], out_sems.at[n]),
                    )
                )
        for load, _ in steps:
            load.start()
        for load, store in steps:
            load.wait()
            store.start()
        for _, store in steps:
            store.wait()


def own_left(high, low, rows):
    return lambda i, a: (high[rows + i, :, lanes(a)], low[rows + i, :, lanes(a)])


def own_kernel(meta, where, kinds, needed, blocks_of, blocks, high, low, total, staged, todo, sems):
    rows = blocks.shape[0]
    tables = (meta, where, kinds, needed, blocks_of)

    @pl.when(meta[0] == 1)
    def _():
        for i in range(rows):
            pltpu.make_async_copy(blocks.at[i], staged.at[i], sems.at[i]).start()
        clear(total)

        def prepare(i, _):
            pltpu.make_async_copy(blocks.at[i], staged.at[i], sems.at[i]).wait()
            split_row(staged.at[i], high.at[rows + i], low.at[rows + i])
            return 0

        lax.fori_loop(0, rows, prepare, 0)
        add_pairs(STAGE_GROUP, (0,), (0, rows), tables, todo, own_left(high, low, rows), high, low, total)


def take_in(pieces, arrived, odd, rows, high, low):
    for (hop, begin), source in zip(pieces, arrived):
        def one(r, _):
            w = window_row(odd, rows, hop, begin, r)
            split_row(source.at[r], high.at[w], low.at[w])
            return 0

        lax.fori_loop(0, source.shape[0], one, 0)


def stage_kernel(sources, pieces, rows, *refs):
    tables, arrived = refs[:5], refs[5 : 5 + len(pieces)]
    high, low, total, todo = refs[5 + len(pieces) + 3 :]

    @pl.when(tables[0][0] == 1)
    def _():
        take_in(pieces, arrived, tables[0][1], rows, high, low)
        add_pairs(STAGE_GROUP, sources, (0, rows), tables, todo, own_left(high, low, rows), high, low, total)


def final_kernel(sources, pieces, part, *refs):
    tables, blocks, arrived = refs[:5], refs[5], refs[6 : 6 + len(pieces)]
    rest = refs[6 + len(pieces) + 3 :]
    high, low, total, keep, other, own, cube, sq_high, sq_low, todo, sem = rest
    rows, width = blocks.shape[0], blocks.shape[1]
    count, share = rows // PIECES, width // 2
    meta = tables[0]
    odd, layer = meta[1], meta[2]
    first = jnp.where(odd == 1, part * count, rows - (part + 1) * count)

    @pl.when(meta[0] == 1)
    def _():
        load = pltpu.make_async_copy(blocks.at[pl.ds(first, count)], own, sem)
        load.start()
        clear(cube)
        take_in(pieces, arrived, odd, rows, high, low)
        add_pairs(PART_GROUP, sources, (first, count), tables, todo, own_left(high, low, rows), high, low, total)
        for i in range(count):
            for s in range(width):
                sq_high[i, s], sq_low[i, s] = halves(total[first + i, s])
        add_pairs(
            CUBE_GROUP, None, (first, count), tables, todo,
            lambda i, a: (sq_high[i, a], sq_low[i, a]), high, low, cube, first,
        )
        load.wait()
        for i in range(count):
            for s in range(share):
                g = layer * share + s
                keep[i, s] = 1.5 * own[i, g] - 0.5 * cube[i, g]
        for i in range(count):
            for s in range(share):
                g = (1 - layer) * share + s
                other[i, s] = 1.5 * own[i, g] - 0.5 * cube[i, g]


def part_begin(meta, rows, part):
    count = rows // PIECES
    return jnp.where(meta[1] == 1, part * count, rows - (part + 1) * count)


def keep_kernel(meta, *refs):
    kept, output, sems = refs[:PIECES], refs[PIECES], refs[PIECES + 1]

    @pl.when(meta[0] == 1)
    def _():
        copies = []
        for part, source in enumerate(kept):
            begin = part_begin(meta, output.shape[0], part)
            target = output.at[pl.ds(begin, source.shape[0])]
            copies.append(pltpu.make_async_copy(source, target, sems.at[part]))
        for copy in copies:
            copy.start()
        for copy in copies:
            copy.wait()


def place_kernel(part, meta, received, output_in, output, sem):
    @pl.when(meta[0] == 0)
    def _():
        begin = part_begin(meta, output.shape[0], part)
        copy = pltpu.make_async_copy(received, output.at[pl.ds(begin, received.shape[0])], sem)
        copy.start()
        copy.wait()


def on_device(cols_n, layers, blocks, columns, row_order):
    rows, width = blocks.shape[0], blocks.shape[1]
    total_rows = row_order.shape[0]
    n = 2 * cols_n
    size = rows // PIECES
    block = (128, 128)
    in_vmem = lambda x: pltpu.with_memory_space_constraint(x, pltpu.VMEM)
    limit = functools.partial(pltpu.CompilerParams, vmem_limit_bytes=20 * 1024 * 1024)

    def device(r, j, l):
        return (r * cols_n + j) * layers + l

    turn = cols_n // 2 // 2 * 2 + 1

    def layer_of(c):
        r, j = divmod(c % n, cols_n)
        return r ^ (j > turn)

    def at_layer(c, l):
        return device(*divmod(c % n, cols_n), l)

    def owner(c, other=0):
        return at_layer(c, layer_of(c) ^ other)

    near = [(at_layer(c, layer_of(c ^ 1)), owner(c ^ 1)) for c in range(n)]
    relay = [(owner(c), owner(c + 2 if c % 2 == 0 else c - 2)) for c in range(n)]
    across = [(owner(c), owner(c, 1)) for c in range(n)]

    r, j, l = (lax.axis_index(a) for a in AXES)
    segment = r * cols_n + j
    odd = segment % 2
    is_owner = ((r == l) != (j > turn)).astype(jnp.int32)
    is_sender = ((r == l) != ((j ^ 1) > turn)).astype(jnp.int32)
    meta = jnp.stack([is_owner, odd, l, is_sender]).astype(jnp.int32)
    held = pltpu.with_memory_space_constraint(blocks, pltpu.HBM)

    piece_shape = jax.ShapeDtypeStruct((size, width) + block, F32)
    first_piece = pl.pallas_call(
        first_kernel,
        out_shape=piece_shape,
        in_specs=[SMEM, ANY],
        out_specs=VMEM,
        scratch_shapes=[pltpu.SemaphoreType.DMA],
        compiler_params=limit(),
        name="cut_first",
    )(meta, held)
    later_pieces = pl.pallas_call(
        cut_kernel,
        out_shape=(piece_shape,) * (PIECES - 1),
        in_specs=[SMEM, ANY, VMEM],
        out_specs=(ANY,) * (PIECES - 1),
        scratch_shapes=[
            pltpu.VMEM((rows - size, width) + block, F32),
            pltpu.SemaphoreType.DMA((rows - size,)),
            pltpu.SemaphoreType.DMA((rows - size,)),
        ],
        compiler_params=limit(),
        name="cut_later",
    )(meta, held, in_vmem(first_piece))
    cuts = (first_piece,) + tuple(later_pieces)
    arrived = {}
    for k in range(PIECES):
        arrived[NEAR, k] = lax.ppermute(cuts[k], AXES, near)
    for k in range(PIECES):
        arrived[FAR, k] = lax.ppermute(arrived[NEAR, k], AXES, relay)

    columns, row_order, arrived[NEAR, 0] = lax.optimization_barrier((columns, row_order, arrived[NEAR, 0]))
    index = jnp.arange(width, dtype=jnp.int32)
    window = (segment * rows - rows + jnp.arange(3 * rows, dtype=jnp.int32)) % total_rows
    window_order, window_cols = row_order[window], columns[window]
    own_cols = lax.dynamic_slice_in_dim(columns, segment * rows, rows, 0)
    same = own_cols[:, :, None] == window_order[None, None, :]
    where = jnp.sum(jnp.where(same, jnp.arange(3 * rows, dtype=jnp.int32), 0), axis=2).reshape(-1)
    named = window_cols[where].reshape(rows, width, width)
    match = named[:, :, :, None] == own_cols[:, None, None, :]
    slots = width + jnp.sum(jnp.where(match, index - width, 0), axis=3).reshape(rows * width, width)
    has = (slots < width).astype(jnp.int32)
    matched = jnp.sum(has, axis=1)
    earlier = jnp.sum(jnp.where(index[None, :, None] > index[None, None, :], has[:, None, :], 0), axis=2)
    rank = jnp.where(has == 1, earlier, matched[:, None] + index - earlier)
    code = 16 * index + slots
    ranked = jnp.sum(jnp.where(rank[:, :, None] == index, code[:, :, None], 0), axis=1)
    blocks_of = jnp.concatenate([ranked.reshape(-1), jnp.full((width,), width, jnp.int32)]).astype(jnp.int32)
    needed = ((matched + 1) // 2).astype(jnp.int32)
    is_own = (where >= rows) & (where < 2 * rows)
    is_near = (where < rows) == (odd == 1)
    inside = where % rows
    piece = jnp.where(odd == 1, inside, rows - 1 - inside) // size
    kinds = jnp.where(is_own, 0, 1 + piece + jnp.where(is_near, 0, PIECES))
    kinds = kinds.astype(jnp.int32)
    where = jnp.concatenate([where, jnp.full((1,), rows, jnp.int32)]).astype(jnp.int32)
    tables = (meta, where, kinds, needed, blocks_of)

    todo = pltpu.SMEM((rows * width * width // 2 + max(STAGE_GROUP, CUBE_GROUP) + width // 2,), jnp.int32)
    state = (
        pltpu.VMEM((3 * rows, 128, width * 128), BF16),
        pltpu.VMEM((3 * rows, 128, width * 128), BF16),
        pltpu.VMEM((rows, width + 1) + block, F32),
    )
    carried = pl.pallas_call(
        own_kernel,
        out_shape=state,
        in_specs=[SMEM] * 5 + [ANY],
        out_specs=(VMEM,) * 3,
        scratch_shapes=[pltpu.VMEM((rows, width) + block, F32), todo, pltpu.SemaphoreType.DMA((rows,))],
        compiler_params=limit(),
        name="own_part",
    )(*tables, held)

    def stage(carried, items):
        m = len(items)
        sources = tuple(1 + k + hop * PIECES for hop, k in items)
        return pl.pallas_call(
            functools.partial(stage_kernel, sources, tuple(items), rows),
            out_shape=state,
            in_specs=[SMEM] * 5 + [VMEM] * (m + 3),
            out_specs=(VMEM,) * 3,
            input_output_aliases={5 + m: 0, 6 + m: 1, 7 + m: 2},
            scratch_shapes=[todo],
            compiler_params=limit(),
        )(*tables, *(in_vmem(arrived[item]) for item in items), *(in_vmem(x) for x in carried))

    part_shape = pltpu.VMEM((size, width // 2) + block, F32)

    def final(carried, items, sources, part):
        m = len(items)
        results = pl.pallas_call(
            functools.partial(final_kernel, sources, tuple(items), part),
            out_shape=state + (part_shape, part_shape),
            in_specs=[SMEM] * 5 + [ANY] + [VMEM] * (m + 3),
            out_specs=(VMEM,) * 5,
            input_output_aliases={6 + m: 0, 7 + m: 1, 8 + m: 2},
            scratch_shapes=[
                pltpu.VMEM((size, width) + block, F32),
                pltpu.VMEM((size, width + 1) + block, F32),
                pltpu.VMEM((size, width) + block, BF16),
                pltpu.VMEM((size, width) + block, BF16),
                todo,
                pltpu.SemaphoreType.DMA,
            ],
            compiler_params=limit(),
        )(*tables, held, *(in_vmem(arrived[item]) for item in items), *(in_vmem(x) for x in carried))
        return results[:3], results[3], results[4]

    carried = stage(carried, [(NEAR, 0), (NEAR, 1), (NEAR, 2), (FAR, 0)])
    kept, got = [], []
    for part in range(PIECES):
        items = [(NEAR, PIECES - 1)] if part == 0 else [(FAR, part)]
        sources = (PIECES,) + tuple(1 + PIECES + k for k in range(1, part + 1))
        carried, keep, give = final(carried, items, sources, part)
        kept.append(keep)
        got.append(lax.ppermute(give, AXES, across))
    output_shape = jax.ShapeDtypeStruct((rows, width // 2) + block, F32)
    output = pl.pallas_call(
        keep_kernel,
        out_shape=output_shape,
        in_specs=[SMEM] + [VMEM] * PIECES,
        out_specs=ANY,
        scratch_shapes=[pltpu.SemaphoreType.DMA((PIECES,))],
        compiler_params=limit(),
        name="keep_parts",
    )(meta, *(in_vmem(x) for x in kept))
    for part in range(PIECES):
        output = pl.pallas_call(
            functools.partial(place_kernel, part),
            out_shape=output_shape,
            in_specs=[SMEM, VMEM, ANY],
            out_specs=ANY,
            input_output_aliases={2: 0},
            scratch_shapes=[pltpu.SemaphoreType.DMA],
            compiler_params=limit(),
        )(meta, in_vmem(got[part]), output)
    return output


def solution(mesh):
    assert mesh.shape["row"] == 2 and mesh.shape["layer"] == 2
    placed = (P(("row", "col"), None, None, None), P(), P())

    def body(*args):
        return on_device(mesh.shape["col"], mesh.shape["layer"], *args)

    return jax.shard_map(
        body,
        mesh=mesh,
        in_specs=placed,
        out_specs=P(("row", "col"), "layer", None, None),
        check_vma=False,
    )
```

```python
import functools

import jax
import jax.numpy as jnp
from jax import lax
from jax.experimental import pallas as pl
from jax.experimental.pallas import tpu as pltpu
from jax.sharding import PartitionSpec as P


AXES = ("row", "col", "layer")
PIECES = 4
OWN_GROUP, STAGE_GROUP, PART_GROUP, CUBE_GROUP = 20, 16, 12, 18
ANY = pl.BlockSpec(memory_space=pl.ANY)
SMEM = pl.BlockSpec(memory_space=pltpu.SMEM)
VMEM = pl.BlockSpec(memory_space=pltpu.VMEM)
F32 = jnp.float32
BF16 = jnp.bfloat16
NEAR, FAR = 0, 1


def halves(x):
    high = x.astype(BF16)
    return high, (x - high.astype(F32)).astype(BF16)


def lanes(t):
    if isinstance(t, int):
        return slice(t * 128, (t + 1) * 128)
    return pl.ds(pl.multiple_of(t * 128, 128), 128)


def split_row(source, high, low):
    for t in range(source.shape[0]):
        high[:, lanes(t)], low[:, lanes(t)] = halves(source[t])


def clear(total):
    def one(i, _):
        for s in range(total.shape[1]):
            total[i, s] = jnp.zeros(total.shape[2:], F32)
        return 0

    lax.fori_loop(0, total.shape[0], one, 0)


def add_pairs(group, sources, span, tables, todo, left, high, low, total, first=0):
    _, where, kinds, needed, blocks_of = tables
    width = total.shape[1] - 1
    twos = width // 2
    pairs = kinds.shape[0]
    start, length = span
    mask = None if sources is None else sum(1 << x for x in sources)

    def list_one(k, count):
        n = start * width + k
        for p in range(twos):
            todo[count + p] = n * twos + p
        more = needed[n]
        return count + (more if mask is None else ((mask >> kinds[n]) & 1) * more)

    count = lax.fori_loop(0, length * width, list_one, jnp.int32(0), unroll=8)
    for k in range(group):
        todo[count + k] = pairs * twos

    def some(m, _):
        for k in range(group):
            entry = todo[m * group + k]
            n = entry // twos
            i = jnp.clip(n // width - first, 0, total.shape[0] - 1)
            w = where[n]
            codes = [blocks_of[2 * entry + e] for e in range(2)]
            left_high, left_low = left(i, n % width)
            right = [jnp.concatenate([x[w, :, lanes(c // 16)] for c in codes], axis=1) for x in (high, low)]
            terms = jnp.dot(
                jnp.concatenate([left_high, left_low, left_high], axis=1),
                jnp.concatenate([right[0], right[0], right[1]], axis=0),
                preferred_element_type=F32,
            )
            for e in range(2):
                total[i, codes[e] % 16] += terms[:, lanes(e)]
        return 0

    lax.fori_loop(0, (count + group - 1) // group, some, 0)


def window_row(odd, rows, hop, begin, r):
    size = rows // PIECES
    ascending, descending = begin * size + r, rows - (begin + 1) * size + r
    before, after = (ascending, 2 * rows + descending) if hop == NEAR else (descending, 2 * rows + ascending)
    return jnp.where(odd == (1 if hop == NEAR else 0), before, after)


def piece_begin(meta, rows, piece):
    size = rows // PIECES
    return jnp.where(meta[1] == 1, rows - (piece + 1) * size, piece * size)


def first_kernel(meta, blocks, out, sem):
    @pl.when(meta[3] == 1)
    def _():
        begin = piece_begin(meta, blocks.shape[0], 0)
        copy = pltpu.make_async_copy(blocks.at[pl.ds(begin, out.shape[0])], out, sem)
        copy.start()
        copy.wait()


def cut_kernel(meta, blocks, first, *rest):
    outs, (staged, in_sems, out_sems) = rest[: PIECES - 1], rest[PIECES - 1 :]
    rows = blocks.shape[0]
    size = rows // PIECES

    @pl.when(meta[3] == 1)
    def _():
        steps = []
        for k, out in enumerate(outs):
            begin = piece_begin(meta, rows, k + 1)
            for r in range(size):
                n = k * size + r
                steps.append(
                    (
                        pltpu.make_async_copy(blocks.at[begin + r], staged.at[n], in_sems.at[n]),
                        pltpu.make_async_copy(staged.at[n], out.at[r], out_sems.at[n]),
                    )
                )
        for load, _ in steps:
            load.start()
        for load, store in steps:
            load.wait()
            store.start()
        for _, store in steps:
            store.wait()


def own_left(high, low, rows):
    return lambda i, a: (high[rows + i, :, lanes(a)], low[rows + i, :, lanes(a)])


def own_kernel(meta, where, kinds, needed, blocks_of, blocks, high, low, total, staged, todo, sems):
    rows = blocks.shape[0]
    tables = (meta, where, kinds, needed, blocks_of)

    @pl.when(meta[0] == 1)
    def _():
        for i in range(rows):
            pltpu.make_async_copy(blocks.at[i], staged.at[i], sems.at[i]).start()
        clear(total)

        def prepare(i, _):
            pltpu.make_async_copy(blocks.at[i], staged.at[i], sems.at[i]).wait()
            split_row(staged.at[i], high.at[rows + i], low.at[rows + i])
            return 0

        lax.fori_loop(0, rows, prepare, 0)
        add_pairs(OWN_GROUP, (0,), (0, rows), tables, todo, own_left(high, low, rows), high, low, total)


def take_in(pieces, arrived, odd, rows, high, low):
    for (hop, begin), source in zip(pieces, arrived):
        def one(r, _):
            w = window_row(odd, rows, hop, begin, r)
            split_row(source.at[r], high.at[w], low.at[w])
            return 0

        lax.fori_loop(0, source.shape[0], one, 0)


def stage_kernel(sources, pieces, rows, *refs):
    tables, arrived = refs[:5], refs[5 : 5 + len(pieces)]
    high, low, total, todo = refs[5 + len(pieces) + 3 :]

    @pl.when(tables[0][0] == 1)
    def _():
        take_in(pieces, arrived, tables[0][1], rows, high, low)
        add_pairs(STAGE_GROUP, sources, (0, rows), tables, todo, own_left(high, low, rows), high, low, total)


def final_kernel(sources, pieces, part, *refs):
    tables, blocks, arrived = refs[:5], refs[5], refs[6 : 6 + len(pieces)]
    rest = refs[6 + len(pieces) + 3 :]
    high, low, total, keep, other, own, cube, sq_high, sq_low, todo, sem = rest
    rows, width = blocks.shape[0], blocks.shape[1]
    count, share = rows // PIECES, width // 2
    meta = tables[0]
    odd, layer = meta[1], meta[2]
    first = jnp.where(odd == 1, part * count, rows - (part + 1) * count)

    @pl.when(meta[0] == 1)
    def _():
        load = pltpu.make_async_copy(blocks.at[pl.ds(first, count)], own, sem)
        load.start()
        clear(cube)
        take_in(pieces, arrived, odd, rows, high, low)
        add_pairs(PART_GROUP, sources, (first, count), tables, todo, own_left(high, low, rows), high, low, total)
        for i in range(count):
            for s in range(width):
                sq_high[i, s], sq_low[i, s] = halves(total[first + i, s])
        add_pairs(
            CUBE_GROUP, None, (first, count), tables, todo,
            lambda i, a: (sq_high[i, a], sq_low[i, a]), high, low, cube, first,
        )
        load.wait()
        for i in range(count):
            for s in range(share):
                g = layer * share + s
                keep[i, s] = 1.5 * own[i, g] - 0.5 * cube[i, g]
        for i in range(count):
            for s in range(share):
                g = (1 - layer) * share + s
                other[i, s] = 1.5 * own[i, g] - 0.5 * cube[i, g]


def part_begin(meta, rows, part):
    count = rows // PIECES
    return jnp.where(meta[1] == 1, part * count, rows - (part + 1) * count)


def keep_kernel(meta, *refs):
    kept, output, sems = refs[:PIECES], refs[PIECES], refs[PIECES + 1]

    @pl.when(meta[0] == 1)
    def _():
        copies = []
        for part, source in enumerate(kept):
            begin = part_begin(meta, output.shape[0], part)
            target = output.at[pl.ds(begin, source.shape[0])]
            copies.append(pltpu.make_async_copy(source, target, sems.at[part]))
        for copy in copies:
            copy.start()
        for copy in copies:
            copy.wait()


def place_kernel(part, meta, received, output_in, output, sem):
    @pl.when(meta[0] == 0)
    def _():
        begin = part_begin(meta, output.shape[0], part)
        copy = pltpu.make_async_copy(received, output.at[pl.ds(begin, received.shape[0])], sem)
        copy.start()
        copy.wait()


def on_device(cols_n, layers, blocks, columns, row_order):
    rows, width = blocks.shape[0], blocks.shape[1]
    total_rows = row_order.shape[0]
    n = 2 * cols_n
    size = rows // PIECES
    block = (128, 128)
    in_vmem = lambda x: pltpu.with_memory_space_constraint(x, pltpu.VMEM)
    limit = functools.partial(pltpu.CompilerParams, vmem_limit_bytes=20 * 1024 * 1024)

    def device(r, j, l):
        return (r * cols_n + j) * layers + l

    turn = cols_n // 2 // 2 * 2 + 1

    def layer_of(c):
        r, j = divmod(c % n, cols_n)
        return r ^ (j > turn)

    def at_layer(c, l):
        return device(*divmod(c % n, cols_n), l)

    def owner(c, other=0):
        return at_layer(c, layer_of(c) ^ other)

    near = [(at_layer(c, layer_of(c ^ 1)), owner(c ^ 1)) for c in range(n)]
    relay = [(owner(c), owner(c + 2 if c % 2 == 0 else c - 2)) for c in range(n)]
    across = [(owner(c), owner(c, 1)) for c in range(n)]

    r, j, l = (lax.axis_index(a) for a in AXES)
    segment = r * cols_n + j
    odd = segment % 2
    is_owner = ((r == l) != (j > turn)).astype(jnp.int32)
    is_sender = ((r == l) != ((j ^ 1) > turn)).astype(jnp.int32)
    meta = jnp.stack([is_owner, odd, l, is_sender]).astype(jnp.int32)
    held = pltpu.with_memory_space_constraint(blocks, pltpu.HBM)

    piece_shape = jax.ShapeDtypeStruct((size, width) + block, F32)
    first_piece = pl.pallas_call(
        first_kernel,
        out_shape=piece_shape,
        in_specs=[SMEM, ANY],
        out_specs=VMEM,
        scratch_shapes=[pltpu.SemaphoreType.DMA],
        compiler_params=limit(),
        name="cut_first",
    )(meta, held)
    later_pieces = pl.pallas_call(
        cut_kernel,
        out_shape=(piece_shape,) * (PIECES - 1),
        in_specs=[SMEM, ANY, VMEM],
        out_specs=(ANY,) * (PIECES - 1),
        scratch_shapes=[
            pltpu.VMEM((rows - size, width) + block, F32),
            pltpu.SemaphoreType.DMA((rows - size,)),
            pltpu.SemaphoreType.DMA((rows - size,)),
        ],
        compiler_params=limit(),
        name="cut_later",
    )(meta, held, in_vmem(first_piece))
    cuts = (first_piece,) + tuple(later_pieces)
    arrived = {}
    for k in range(PIECES):
        arrived[NEAR, k] = lax.ppermute(cuts[k], AXES, near)
    for k in range(PIECES):
        arrived[FAR, k] = lax.ppermute(arrived[NEAR, k], AXES, relay)

    columns, row_order, arrived[NEAR, 0] = lax.optimization_barrier((columns, row_order, arrived[NEAR, 0]))
    index = jnp.arange(width, dtype=jnp.int32)
    window = (segment * rows - rows + jnp.arange(3 * rows, dtype=jnp.int32)) % total_rows
    window_order, window_cols = row_order[window], columns[window]
    own_cols = lax.dynamic_slice_in_dim(columns, segment * rows, rows, 0)
    same = own_cols[:, :, None] == window_order[None, None, :]
    where = jnp.sum(jnp.where(same, jnp.arange(3 * rows, dtype=jnp.int32), 0), axis=2).reshape(-1)
    named = window_cols[where].reshape(rows, width, width)
    match = named[:, :, :, None] == own_cols[:, None, None, :]
    slots = width + jnp.sum(jnp.where(match, index - width, 0), axis=3).reshape(rows * width, width)
    has = (slots < width).astype(jnp.int32)
    matched = jnp.sum(has, axis=1)
    earlier = jnp.sum(jnp.where(index[None, :, None] > index[None, None, :], has[:, None, :], 0), axis=2)
    rank = jnp.where(has == 1, earlier, matched[:, None] + index - earlier)
    code = 16 * index + slots
    ranked = jnp.sum(jnp.where(rank[:, :, None] == index, code[:, :, None], 0), axis=1)
    blocks_of = jnp.concatenate([ranked.reshape(-1), jnp.full((width,), width, jnp.int32)]).astype(jnp.int32)
    needed = ((matched + 1) // 2).astype(jnp.int32)
    is_own = (where >= rows) & (where < 2 * rows)
    is_near = (where < rows) == (odd == 1)
    inside = where % rows
    piece = jnp.where(odd == 1, inside, rows - 1 - inside) // size
    kinds = jnp.where(is_own, 0, 1 + piece + jnp.where(is_near, 0, PIECES))
    kinds = kinds.astype(jnp.int32)
    where = jnp.concatenate([where, jnp.full((1,), rows, jnp.int32)]).astype(jnp.int32)
    tables = (meta, where, kinds, needed, blocks_of)

    todo = pltpu.SMEM((rows * width * width // 2 + max(OWN_GROUP, STAGE_GROUP, PART_GROUP, CUBE_GROUP) + width // 2,), jnp.int32)
    state = (
        pltpu.VMEM((3 * rows, 128, width * 128), BF16),
        pltpu.VMEM((3 * rows, 128, width * 128), BF16),
        pltpu.VMEM((rows, width + 1) + block, F32),
    )
    carried = pl.pallas_call(
        own_kernel,
        out_shape=state,
        in_specs=[SMEM] * 5 + [ANY],
        out_specs=(VMEM,) * 3,
        scratch_shapes=[pltpu.VMEM((rows, width) + block, F32), todo, pltpu.SemaphoreType.DMA((rows,))],
        compiler_params=limit(),
        name="own_part",
    )(*tables, held)

    def stage(carried, items):
        m = len(items)
        sources = tuple(1 + k + hop * PIECES for hop, k in items)
        return pl.pallas_call(
            functools.partial(stage_kernel, sources, tuple(items), rows),
            out_shape=state,
            in_specs=[SMEM] * 5 + [VMEM] * (m + 3),
            out_specs=(VMEM,) * 3,
            input_output_aliases={5 + m: 0, 6 + m: 1, 7 + m: 2},
            scratch_shapes=[todo],
            compiler_params=limit(),
        )(*tables, *(in_vmem(arrived[item]) for item in items), *(in_vmem(x) for x in carried))

    part_shape = pltpu.VMEM((size, width // 2) + block, F32)

    def final(carried, items, sources, part):
        m = len(items)
        results = pl.pallas_call(
            functools.partial(final_kernel, sources, tuple(items), part),
            out_shape=state + (part_shape, part_shape),
            in_specs=[SMEM] * 5 + [ANY] + [VMEM] * (m + 3),
            out_specs=(VMEM,) * 5,
            input_output_aliases={6 + m: 0, 7 + m: 1, 8 + m: 2},
            scratch_shapes=[
                pltpu.VMEM((size, width) + block, F32),
                pltpu.VMEM((size, width + 1) + block, F32),
                pltpu.VMEM((size, width) + block, BF16),
                pltpu.VMEM((size, width) + block, BF16),
                todo,
                pltpu.SemaphoreType.DMA,
            ],
            compiler_params=limit(),
        )(*tables, held, *(in_vmem(arrived[item]) for item in items), *(in_vmem(x) for x in carried))
        return results[:3], results[3], results[4]

    carried = stage(carried, [(NEAR, 0), (NEAR, 1), (NEAR, 2), (FAR, 0)])
    kept, got = [], []
    for part in range(PIECES):
        items = [(NEAR, PIECES - 1)] if part == 0 else [(FAR, part)]
        sources = (PIECES,) + tuple(1 + PIECES + k for k in range(1, part + 1))
        carried, keep, give = final(carried, items, sources, part)
        kept.append(keep)
        got.append(lax.ppermute(give, AXES, across))
    output_shape = jax.ShapeDtypeStruct((rows, width // 2) + block, F32)
    output = pl.pallas_call(
        keep_kernel,
        out_shape=output_shape,
        in_specs=[SMEM] + [VMEM] * PIECES,
        out_specs=ANY,
        scratch_shapes=[pltpu.SemaphoreType.DMA((PIECES,))],
        compiler_params=limit(),
        name="keep_parts",
    )(meta, *(in_vmem(x) for x in kept))
    for part in range(PIECES):
        output = pl.pallas_call(
            functools.partial(place_kernel, part),
            out_shape=output_shape,
            in_specs=[SMEM, VMEM, ANY],
            out_specs=ANY,
            input_output_aliases={2: 0},
            scratch_shapes=[pltpu.SemaphoreType.DMA],
            compiler_params=limit(),
        )(meta, in_vmem(got[part]), output)
    return output


def solution(mesh):
    assert mesh.shape["row"] == 2 and mesh.shape["layer"] == 2
    placed = (P(("row", "col"), None, None, None), P(), P())

    def body(*args):
        return on_device(mesh.shape["col"], mesh.shape["layer"], *args)

    return jax.shard_map(
        body,
        mesh=mesh,
        in_specs=placed,
        out_specs=P(("row", "col"), "layer", None, None),
        check_vma=False,
    )
```
